32 devices in a mesh: sector: 4 (over y, x), term: 8 (over z, core).
Axes of the slice: x: 2, y: 2, z: 4, core: 2. Of those that a mesh axis runs over, the one named last changes fastest.
Arguments:
- wavefunction: float32 [4, 256, 256], P('sector'), may hold values from -6 to 6
- left_env: float32 [384, 256, 256], P(('sector', 'term')), may hold values from -0.0390625 to 0.0390625
- right_env: float32 [384, 256, 256], P(('sector', 'term')), may hold values from -0.375 to 0.375
- in_sector: int32 [384], P(('sector', 'term')), may hold values from 0 to 3
- out_sector: int32 [384], P(('sector', 'term')), may hold values from 0 to 3
- precond: float32 [4, 256, 256], P('sector'), may hold values from 2 to 4
- shifts: float32 [2], replicated, may hold values from 0.2 to 1
Outputs:
- corrected: float32 [4, 256, 256], P('sector')
- residual_norms: float32 [2], replicated
The draws below stay inside these ranges and needn't reach their ends.
All inputs are finite; a program needn't handle non-finite values.
Results may differ from the reference program's by a relative error of at most 0.0001.
Values sent between devices are 32-bit elements; how exact they have to be, the bound alone decides.
A program may use at most 64 MiB of HBM per device.

```python
import math
import jax
import jax.numpy as jnp
import numpy as np
from jax import lax

B = 256
SEC_DEV = 1
TASK_DEV = 12
ITERS = 2
SECTORS = 4
TASKS = 384
N_TERM = 8


def touch_ends(drawn, own_key, smallest, top_value):
    spot = [jax.random.randint(jax.random.fold_in(own_key, axis), (), 0, length) for axis, length in enumerate(drawn.shape)]
    main_axis = drawn.shape.index(max(drawn.shape))
    next_to = spot[:main_axis] + [(spot[main_axis] + 1) % drawn.shape[main_axis]] + spot[main_axis + 1:]
    return drawn.at[tuple(spot)].set(smallest).at[tuple(next_to)].set(top_value)


def block_scale(rng, dims, pieces, low, high):
    def one(position, shards_of):
        heights = jax.random.uniform(jax.random.fold_in(jax.random.fold_in(rng, 6), position), (shards_of,), jnp.float32, low / len(pieces), high / len(pieces))
        return jnp.repeat(jnp.exp(heights), dims[position] // shards_of).reshape((-1,) + (1,) * (len(dims) - position - 1))

    factor_of = one(*pieces[0])
    for cut in pieces[1:]:
        factor_of = factor_of * one(*cut)
    return factor_of


def cumulative_ranks(amount, slope):
    loads = [(1 << 20) // math.isqrt(rank ** slope) + 1 for rank in range(1, amount + 1)]
    scale = 1 + sum(loads) // (1 << 30)
    return np.cumsum(np.array([max(1, weight // scale) for weight in loads]))


def ranked(rng, dims, count, lean):
    listing = cumulative_ranks(count, lean)
    lot = jax.random.randint(jax.random.fold_in(rng, 1), dims, 0, int(listing[count - 1]))
    rank = jnp.searchsorted(jnp.asarray(listing, jnp.int32), lot, side="right")
    return jax.random.permutation(jax.random.fold_in(rng, 2), count)[rank].astype(jnp.int32)


def scatter_about(key, dims, spread, bound, pieces=(), held_as=jnp.bfloat16):
    entries = spread * jax.random.normal(key, dims, jnp.float32)
    if pieces:
        entries = entries * block_scale(key, dims, pieces, -0.22, 0.18)
    return jnp.clip(entries, -bound, bound).astype(held_as)


def setup_inputs(seed: int = 0) -> dict:
    keys = jax.random.split(jax.random.key(seed), 8)
    wavefunction = scatter_about(keys[0], (SECTORS, B, B), 1.0, 6.0, ((0, 4),), jnp.float32)
    left_env = scatter_about(keys[1], (TASKS, B, B), (B * TASK_DEV * N_TERM // SEC_DEV) ** -0.5, 0.0390625, ((0, 32),), jnp.float32)
    right_env = scatter_about(keys[2], (TASKS, B, B), B ** -0.5, 0.375, ((0, 32),), jnp.float32)
    in_sector = touch_ends(ranked(keys[3], (TASKS,), SECTORS, 1), jax.random.fold_in(keys[3], 3), 0, SECTORS - 1).astype(jnp.int32)
    out_sector = touch_ends(jax.random.randint(keys[4], (TASKS,), 0, SECTORS), jax.random.fold_in(keys[4], 1), 0, SECTORS - 1).astype(jnp.int32)
    precond = jnp.clip(2.0 + 2.0 * jax.random.uniform(keys[5], (SECTORS, B, B), jnp.float32) ** block_scale(keys[5], (SECTORS, B, B), ((0, 4),), -0.2, 0.2), 2.0, 4.0)
    shifts = jnp.clip(jax.random.uniform(keys[6], (ITERS,), jnp.float32, 0.2, 1.0), 0.2, 1.0)
    return {"wavefunction": wavefunction, "left_env": left_env, "right_env": right_env, "in_sector": in_sector, "out_sector": out_sector, "precond": precond, "shifts": shifts}


def apply_tasks(full, left_env, right_env, in_sector, out_sector):

    def one_task(total, item):
        left, right, source, target = item
        block = lax.dynamic_index_in_dim(full, source, 0, keepdims=False)
        middle = jnp.dot(left, block, precision=lax.Precision.HIGHEST, preferred_element_type=jnp.float32)
        result = jnp.dot(middle, right, precision=lax.Precision.HIGHEST, preferred_element_type=jnp.float32)
        current = lax.dynamic_index_in_dim(total, target, 0, keepdims=False)
        total = lax.dynamic_update_index_in_dim(total, current + result, target, 0)
        return (total, None)
    start = jnp.zeros(full.shape, jnp.float32)
    total, _ = lax.scan(one_task, start, (left_env, right_env, in_sector, out_sector))
    return total

def reference(wavefunction, left_env, right_env, in_sector, out_sector, precond, shifts):
    psi = wavefunction
    norms = []
    for step in range(ITERS):
        sigma = apply_tasks(psi, left_env, right_env, in_sector, out_sector)
        residual = sigma - shifts[step] * psi
        norms.append(jnp.sqrt(jnp.sum(residual * residual)))
        updated = psi - residual / (precond - shifts[step])
        psi = updated / jnp.sqrt(jnp.mean(updated * updated) + 1e-06)
    return (psi, jnp.stack(norms))
```

```python
import functools

import jax
import jax.numpy as jnp
from jax import lax
from jax.experimental import pallas as pl
from jax.experimental.pallas import tpu as pltpu
from jax.sharding import PartitionSpec as P

F32 = jnp.float32
BF16 = jnp.bfloat16


def split(x):
    hi = x.astype(BF16)
    return hi, (x - hi.astype(F32)).astype(BF16)


def rcopy(src, dst, sems, at, dev):
    return pltpu.make_async_remote_copy(
        src_ref=src,
        dst_ref=dst,
        send_sem=sems[0].at[at],
        recv_sem=sems[1].at[at],
        device_id=dev,
        device_id_type=pl.DeviceIdType.MESH,
    )


def each(start, stop, body):
    lax.fori_loop(start, stop, lambda i, _: (body(i), 0)[1], 0)


def kernel(
    S, T,
    in_s, out_s, shifts, wf, pre, left, right,
    out, norms,
    stage, env, full, fin, psi, mid, res, part, p1r, p2r, zsum, p3r, stat, zsr, xsr, csr,
    esem, *sems,
):
    g0, f0, p1, p2, p3, zg, xg, cg, zst, xst, cst = [
        (sems[2 * i], sems[2 * i + 1]) for i in range(len(sems) // 2)
    ]
    n_task, B = left.shape[0], wf.shape[-1]
    iters = norms.shape[0]
    Z, H = T // 2, B // 2
    R = H // Z
    count = S * B * B
    ms, mt = lax.axis_index("sector"), lax.axis_index("term")
    mz, mc = mt // 2, lax.rem(mt, 2)

    def sec_to(k):
        return lax.rem(ms + k, S)

    def sec_from(k):
        return lax.rem(ms + S - k, S)

    def z_to(k):
        return lax.rem(mz + k, Z)

    def z_from(k):
        return lax.rem(mz + Z - k, Z)

    def xy_dev(k):
        return (sec_to(k), mt)

    def z_dev(k):
        return (ms, z_to(k) * 2 + mc)

    core_dev = (ms, mz * 2 + 1 - mc)

    def half(c):
        return pl.ds(pl.multiple_of(c * H, H), H)

    def piece(c, z):
        return pl.ds(pl.multiple_of(c * H + z * R, R), R)

    def zrows(z):
        return pl.ds(pl.multiple_of(z * R, R), R)

    def env_copy(which, t):
        src = left if which == 0 else right
        return pltpu.make_async_copy(src.at[t], stage.at[which, t], esem.at[which, t])

    for which in range(2):
        each(0, n_task, lambda t: env_copy(which, t).start())

    barrier = pltpu.get_barrier_semaphore()

    def greet(dev):
        pl.semaphore_signal(barrier, inc=1, device_id=dev, device_id_type=pl.DeviceIdType.MESH)

    each(1, S, lambda k: greet(xy_dev(k)))
    each(1, Z, lambda k: greet(z_dev(k)))
    greet(core_dev)
    pl.semaphore_wait(barrier, S + Z - 1)

    def g0_copy(k):
        return rcopy(wf.at[0, half(mc)], full.at[0, ms, half(mc)], g0, k, xy_dev(k))

    def g0_in(k):
        here = full.at[0, sec_from(k), half(mc)]
        return rcopy(here, here, g0, k, xy_dev(k))

    def f0_copy(k):
        here = full.at[0, sec_from(k), half(mc)]
        return rcopy(here, here, f0, k, core_dev)

    def f0_in(k):
        here = full.at[0, sec_from(k), half(1 - mc)]
        return rcopy(here, here, f0, k, core_dev)

    each(1, S, lambda k: g0_copy(k).start())

    CH = 32

    def split_rows(load, dst, s):
        def rows(i):
            at = pl.ds(pl.multiple_of(i * CH, CH), CH)
            hi, lo = split(load(at))
            dst[0, s, at, :] = hi
            dst[1, s, at, :] = lo

        each(0, B // CH, rows)

    split_rows(lambda at: wf[0, at, :], psi, ms)

    for which in range(2):
        def convert(t):
            env_copy(which, t).wait()
            split_rows(lambda at: stage[which, t, at, :], env.at[which], t)

        each(0, n_task, convert)

    def forward0(k):
        g0_in(k).wait_recv()
        f0_copy(k).start()

    each(1, S, forward0)

    def arrive0(k):
        f0_in(k).wait_recv()
        s = sec_from(k)
        split_rows(lambda at: full[0, s, at, :], psi, s)

    each(1, S, arrive0)

    scale = None
    for it in range(iters):
        last = it == iters - 1

        def first(t):
            s = in_s[t]
            lh, ll = env[0, 0, t], env[0, 1, t]
            ph, plo = psi[0, s], psi[1, s]
            m = jnp.dot(
                jnp.concatenate([lh, ll, lh], axis=1),
                jnp.concatenate([ph, ph, plo], axis=0),
                preferred_element_type=F32,
            )
            mid[0, t], mid[1, t] = split(m)

        def second(t):
            mh, ml = mid[0, t], mid[1, t]
            rh, rl = env[1, 0, t], env[1, 1, t]
            res[t] = jnp.dot(
                jnp.concatenate([mh, ml, mh], axis=1),
                jnp.concatenate([rh, rh, rl], axis=0),
                preferred_element_type=F32,
            )

        each(0, n_task, first)
        each(0, n_task, second)

        def sums(s, c, dst, extra):
            coef = [jnp.where(out_s[t] == s, 1.0, 0.0).astype(F32) for t in range(n_task)]

            def rows(i):
                at = pl.ds(pl.multiple_of(i * CH, CH), CH)
                src = pl.ds(pl.multiple_of(c * H + i * CH, CH), CH)
                total = coef[0] * res[0, src, :]
                for t in range(1, n_task):
                    total = total + coef[t] * res[t, src, :]
                if extra:
                    total = total + p1r[it, s, at, :]
                part[dst, s, at, :] = total

            each(0, H // CH, rows)

        def p1_copy(s):
            return rcopy(part.at[1, s], p1r.at[it, s], p1, (it, s), core_dev)

        def to_partner(k):
            s = sec_to(k)
            sums(s, 1 - mc, 1, False)
            p1_copy(s).start()

        each(1, S + 1, to_partner)

        def p2_copy(j, k):
            return rcopy(
                part.at[0, sec_to(j), zrows(z_to(k))], p2r.at[it, j, k], p2, (it, j, k), xy_dev(j)
            )

        def to_owner(j):
            s = sec_to(j)
            p1_copy(s).wait_recv()
            sums(s, mc, 0, True)
            each(1, Z + 1, lambda k: p2_copy(j, lax.rem(k, Z)).start())

        each(1, S, to_owner)
        p1_copy(ms).wait_recv()
        sums(ms, mc, 0, True)

        def piece_sum(k):
            total = part[0, ms, zrows(z_to(k)), :]
            for j in range(1, S):
                p2_copy(j, k).wait_recv()
                total = total + p2r[it, j, k]
            return total

        def p3_copy(k):
            return rcopy(zsum.at[k], p3r.at[it, k], p3, (it, k), z_dev(k))

        def to_z(k):
            zsum[k] = piece_sum(k)
            p3_copy(k).start()

        each(1, Z, to_z)
        sigma = piece_sum(0)
        for k in range(1, Z):
            p3_copy(k).wait_recv()
            sigma = sigma + p3r[it, k]

        mine = piece(mc, mz)
        shift = shifts[it]
        prev = wf[0, mine, :] if it == 0 else full[it, ms, mine, :]
        residual = sigma - shift * prev
        updated = prev - residual / (pre[0, mine, :] - shift)
        res_sq = jnp.sum(residual * residual, axis=(0, 1), keepdims=True)
        upd_sq = jnp.sum(updated * updated, axis=(0, 1), keepdims=True)
        row = lax.broadcasted_iota(jnp.int32, (8, 128), 0)
        tile = jnp.where(row < 4, res_sq, upd_sq)

        def spot(s, at):
            return fin.at[at] if last else full.at[it + 1, s, at]

        if last:
            fin[mine, :] = updated
        else:
            full[it + 1, ms, mine, :] = updated
        stat[it, 0] = tile

        def zst_copy(k):
            return rcopy(stat.at[it, 0], zsr.at[it, k], zst, (it, k), z_dev(k))

        def xst_copy(j):
            return rcopy(stat.at[it, 1], xsr.at[it, j], xst, (it, j), xy_dev(j))

        cst_copy = rcopy(stat.at[it, 2], csr.at[it], cst, it, core_dev)

        def zg_copy(k):
            return rcopy(spot(ms, mine), spot(ms, mine), zg, (it, k), z_dev(k))

        def zg_in(k):
            here = spot(ms, piece(mc, z_from(k)))
            return rcopy(here, here, zg, (it, k), z_dev(k))

        def xg_copy(j, k):
            here = spot(ms, piece(mc, z_from(k)))
            return rcopy(here, here, xg, (it, j, k), xy_dev(j))

        def xg_in(j, k):
            here = spot(sec_from(j), piece(mc, z_from(k)))
            return rcopy(here, here, xg, (it, j, k), xy_dev(j))

        def cg_copy(j, k):
            here = spot(sec_from(j), piece(mc, z_from(k)))
            return rcopy(here, here, cg, (it, j, k), core_dev)

        def cg_in(j, k):
            here = spot(sec_from(j), piece(1 - mc, z_from(k)))
            return rcopy(here, here, cg, (it, j, k), core_dev)

        def spread(k):
            if not last:
                each(1, S, lambda j: xg_copy(j, k).start())
            cg_copy(0, k).start()

        each(1, Z, lambda k: zst_copy(k).start())
        each(1, Z, lambda k: zg_copy(k).start())
        spread(0)
        for k in range(1, Z):
            zst_copy(k).wait_recv()
            tile = tile + zsr[it, k]
        stat[it, 1] = tile
        each(1, S, lambda j: xst_copy(j).start())

        def relay_z(k):
            zg_in(k).wait_recv()
            spread(k)

        each(1, Z, relay_z)

        for j in range(1, S):
            xst_copy(j).wait_recv()
            tile = tile + xsr[it, j]
        stat[it, 2] = tile
        cst_copy.start()

        if not last:
            def relay_xy(k):
                def one(j):
                    xg_in(j, k).wait_recv()
                    cg_copy(j, k).start()

                each(1, S, one)

            each(0, Z, relay_xy)

        cst_copy.wait_recv()
        tile = tile + csr[it]
        res_all, upd_all = tile[0:1, 0:1], tile[4:5, 0:1]
        norm = jnp.sqrt(res_all)
        mean = upd_all / count
        if scale is None:
            scale = 1.0 / jnp.sqrt(mean + 1e-06)
        else:
            norm = norm * scale
            scale = scale / jnp.sqrt(scale * scale * mean + 1e-06)
        norms[it] = norm[0, 0]

        if last:
            each(0, Z, lambda k: cg_in(0, k).wait_recv())
            out[0] = fin[...] * scale
        else:
            def arrive(j):
                each(0, Z, lambda k: cg_in(j, k).wait_recv())
                s = sec_from(j)
                split_rows(lambda at: full[it + 1, s, at, :], psi, s)

            each(0, S, arrive)

        if it == 0:
            each(1, S, lambda k: g0_copy(k).wait_send())
            each(1, S, lambda k: f0_copy(k).wait_send())
        each(0, S, lambda s: p1_copy(s).wait_send())
        each(1, S, lambda j: each(0, Z, lambda k: p2_copy(j, k).wait_send()))
        each(1, Z, lambda k: p3_copy(k).wait_send())
        each(1, Z, lambda k: zst_copy(k).wait_send())
        each(1, S, lambda j: xst_copy(j).wait_send())
        cst_copy.wait_send()
        each(1, Z, lambda k: zg_copy(k).wait_send())
        each(0, Z, lambda k: cg_copy(0, k).wait_send())
        if not last:
            each(1, S, lambda j: each(0, Z, lambda k: xg_copy(j, k).wait_send()))
            each(1, S, lambda j: each(0, Z, lambda k: cg_copy(j, k).wait_send()))


def per_device(S, T, wavefunction, left_env, right_env, in_sector, out_sector, precond, shifts):
    n_task, B = left_env.shape[0], left_env.shape[-1]
    iters = shifts.shape[0]
    Z, H = T // 2, B // 2
    R = H // Z
    dma = pltpu.SemaphoreType.DMA
    vmem = pl.BlockSpec(memory_space=pltpu.VMEM)
    smem = pl.BlockSpec(memory_space=pltpu.SMEM)
    hbm = pl.BlockSpec(memory_space=pl.ANY)
    sem_shapes = [
        (S,), (S,), (iters, S), (iters, S, Z), (iters, Z), (iters, Z),
        (iters, S, Z), (iters, S, Z), (iters, Z), (iters, S), (iters,),
    ]
    return pl.pallas_call(
        functools.partial(kernel, S, T),
        out_shape=(
            jax.ShapeDtypeStruct((1, B, B), F32),
            jax.ShapeDtypeStruct((iters,), F32),
        ),
        in_specs=[smem, smem, smem, vmem, vmem, hbm, hbm],
        out_specs=(vmem, smem),
        scratch_shapes=[
            pltpu.VMEM((2, n_task, B, B), F32),
            pltpu.VMEM((2, 2, n_task, B, B), BF16),
            pltpu.VMEM((iters, S, B, B), F32),
            pltpu.VMEM((B, B), F32),
            pltpu.VMEM((2, S, B, B), BF16),
            pltpu.VMEM((2, n_task, B, B), BF16),
            pltpu.VMEM((n_task, B, B), F32),
            pltpu.VMEM((2, S, H, B), F32),
            pltpu.VMEM((iters, S, H, B), F32),
            pltpu.VMEM((iters, S, Z, R, B), F32),
            pltpu.VMEM((Z, R, B), F32),
            pltpu.VMEM((iters, Z, R, B), F32),
            pltpu.VMEM((iters, 3, 8, 128), F32),
            pltpu.VMEM((iters, Z, 8, 128), F32),
            pltpu.VMEM((iters, S, 8, 128), F32),
            pltpu.VMEM((iters, 8, 128), F32),
            dma((2, n_task)),
        ]
        + [dma(shape) for shape in sem_shapes for _ in range(2)],
        compiler_params=pltpu.CompilerParams(
            collective_id=0, has_side_effects=True, vmem_limit_bytes=62 * 1024 * 1024
        ),
    )(in_sector, out_sector, shifts, wavefunction, precond, left_env, right_env)


def solution(mesh):
    placed = (
        P("sector", None, None),
        P(("sector", "term"), None, None),
        P(("sector", "term"), None, None),
        P(("sector", "term")),
        P(("sector", "term")),
        P("sector", None, None),
        P(),
    )
    return jax.shard_map(
        functools.partial(per_device, mesh.shape["sector"], mesh.shape["term"]),
        mesh=mesh,
        in_specs=placed,
        out_specs=(P("sector", None, None), P()),
        check_vma=False,
    )
```

```python
import functools

import jax
import jax.numpy as jnp
from jax import lax
from jax.experimental import pallas as pl
from jax.experimental.pallas import tpu as pltpu
from jax.sharding import PartitionSpec as P

F32 = jnp.float32
BF16 = jnp.bfloat16


def split(x):
    hi = x.astype(BF16)
    return hi, (x - hi.astype(F32)).astype(BF16)


def rcopy(src, dst, sems, out_at, in_at, dev):
    return pltpu.make_async_remote_copy(
        src_ref=src,
        dst_ref=dst,
        send_sem=sems[0].at[out_at],
        recv_sem=sems[1].at[in_at],
        device_id=dev,
        device_id_type=pl.DeviceIdType.MESH,
    )


def each(start, stop, body):
    if stop - start <= 4:
        for i in range(start, stop):
            body(i)
    else:
        lax.fori_loop(start, stop, lambda i, _: (body(i), 0)[1], 0)


def kernel(
    S, T,
    in_s, out_s, shifts, wf, pre, left, right,
    out, norms,
    stage, env, full, fin, psi, mid, res, part, p1r, p2r, zsum, p3r, stat, zsr, xsr,
    esem, *sems,
):
    g0, f0, p1, p2, p3, zg, xg, cg, zst, xst = [
        (sems[2 * i], sems[2 * i + 1]) for i in range(len(sems) // 2)
    ]
    n_task, B = left.shape[0], wf.shape[-1]
    iters = norms.shape[0]
    Z, H = T // 2, B // 2
    R = H // Z
    count = S * B * B
    ms, mt = lax.axis_index("sector"), lax.axis_index("term")
    mz, mc = mt // 2, lax.rem(mt, 2)

    def sec_to(k):
        return lax.rem(ms + k, S)

    def sec_from(k):
        return lax.rem(ms + S - k, S)

    def z_to(k):
        return lax.rem(mz + k, Z)

    def z_from(k):
        return lax.rem(mz + Z - k, Z)

    def xy_dev(k):
        return (sec_to(k), mt)

    def z_dev(k):
        return (ms, z_to(k) * 2 + mc)

    def term_dev(k):
        return (ms, lax.rem(mt + k, T))

    core_dev = (ms, mz * 2 + 1 - mc)

    def half(c):
        return pl.ds(pl.multiple_of(c * H, H), H)

    def piece(c, z):
        return pl.ds(pl.multiple_of(c * H + z * R, R), R)

    def zrows(z):
        return pl.ds(pl.multiple_of(z * R, R), R)

    def env_copy(which, t):
        src = left if which == 0 else right
        return pltpu.make_async_copy(src.at[t], stage.at[which, t], esem.at[which, t])

    for which in range(2):
        each(0, n_task, lambda t: env_copy(which, t).start())

    barrier = pltpu.get_barrier_semaphore()

    def greet(dev):
        pl.semaphore_signal(barrier, inc=1, device_id=dev, device_id_type=pl.DeviceIdType.MESH)

    each(1, S, lambda k: greet(xy_dev(k)))
    for k in range(1, T):
        greet(term_dev(k))
    pl.semaphore_wait(barrier, S + T - 2)

    def g0_copy(k):
        return rcopy(wf.at[0, half(mc)], full.at[0, ms, half(mc)], g0, 0, k, xy_dev(k))

    def g0_in(k):
        here = full.at[0, sec_from(k), half(mc)]
        return rcopy(here, here, g0, 0, k, xy_dev(k))

    def f0_copy(k):
        here = full.at[0, sec_from(k), half(mc)]
        return rcopy(here, here, f0, 0, k, core_dev)

    def f0_in(k):
        here = full.at[0, sec_from(k), half(1 - mc)]
        return rcopy(here, here, f0, 0, k, core_dev)

    each(1, S, lambda k: g0_copy(k).start())

    CH = 32

    def split_rows(load, dst, s):
        def rows(i):
            at = pl.ds(pl.multiple_of(i * CH, CH), CH)
            hi, lo = split(load(at))
            dst[0, s, at, :] = hi
            dst[1, s, at, :] = lo

        each(0, B // CH, rows)

    split_rows(lambda at: wf[0, at, :], psi, ms)

    for which in range(2):
        def convert(t):
            env_copy(which, t).wait()
            split_rows(lambda at: stage[which, t, at, :], env.at[which], t)

        each(0, n_task, convert)

    def forward0(k):
        g0_in(k).wait_recv()
        f0_copy(k).start()

    each(1, S, forward0)

    def arrive0(k):
        f0_in(k).wait_recv()
        s = sec_from(k)
        split_rows(lambda at: full[0, s, at, :], psi, s)

    each(1, S, arrive0)

    tile = jnp.zeros((8, 128), F32)
    for it in range(iters):
        last = it == iters - 1

        def first(t):
            s = in_s[t]
            lh, ll = env[0, 0, t], env[0, 1, t]
            ph, plo = psi[0, s], psi[1, s]
            m = jnp.dot(
                jnp.concatenate([lh, ll, lh], axis=1),
                jnp.concatenate([ph, ph, plo], axis=0),
                preferred_element_type=F32,
            )
            mid[0, t], mid[1, t] = split(m)

        def second(t):
            mh, ml = mid[0, t], mid[1, t]
            rh, rl = env[1, 0, t], env[1, 1, t]
            res[t] = jnp.dot(
                jnp.concatenate([mh, ml, mh], axis=1),
                jnp.concatenate([rh, rh, rl], axis=0),
                preferred_element_type=F32,
            )

        for t in range(n_task):
            first(t)
        for t in range(n_task):
            second(t)

        def sums(s, c, dst, extra):
            coef = [jnp.where(out_s[t] == s, 1.0, 0.0).astype(F32) for t in range(n_task)]

            def rows(i):
                at = pl.ds(pl.multiple_of(i * CH, CH), CH)
                src = pl.ds(pl.multiple_of(c * H + i * CH, CH), CH)
                total = coef[0] * res[0, src, :]
                for t in range(1, n_task):
                    total = total + coef[t] * res[t, src, :]
                if extra:
                    total = total + p1r[it, s, at, :]
                part[dst, s, at, :] = total

            each(0, H // CH, rows)

        def p1_copy(s):
            return rcopy(part.at[1, s], p1r.at[it, s], p1, it, (it, s), core_dev)

        def to_partner(k):
            s = sec_to(k)
            sums(s, 1 - mc, 1, False)
            p1_copy(s).start()

        each(1, S + 1, to_partner)

        def p2_copy(j, k):
            return rcopy(
                part.at[0, sec_to(j), zrows(z_to(k))], p2r.at[it, k, j], p2, it, (it, k), xy_dev(j)
            )

        def to_owner(j):
            s = sec_to(j)
            p1_copy(s).wait_recv()
            sums(s, mc, 0, True)
            each(1, Z + 1, lambda k: p2_copy(j, lax.rem(k, Z)).start())

        each(1, S, to_owner)
        p1_copy(ms).wait_recv()
        sums(ms, mc, 0, True)

        def piece_sum(k):
            total = part[0, ms, zrows(z_to(k)), :]
            here = p2r.at[it, k, pl.ds(1, S - 1)]
            rcopy(here, here, p2, it, (it, k), xy_dev(1)).wait_recv()
            for j in range(1, S):
                total = total + p2r[it, k, j]
            return total

        def p3_copy(k):
            return rcopy(zsum.at[k], p3r.at[it, k], p3, it, (it, k), z_dev(k))

        def to_z(k):
            zsum[k] = piece_sum(k)
            p3_copy(k).start()

        each(1, Z, to_z)
        sigma = piece_sum(0)
        for k in range(1, Z):
            p3_copy(k).wait_recv()
            sigma = sigma + p3r[it, k]

        mine = piece(mc, mz)
        shift = shifts[it]
        prev = wf[0, mine, :] if it == 0 else full[it, ms, mine, :]
        residual = sigma - shift * prev
        updated = prev - residual / (pre[0, mine, :] - shift)
        res_sq = jnp.sum(residual * residual, axis=(0, 1), keepdims=True)
        upd_sq = jnp.sum(updated * updated, axis=(0, 1), keepdims=True)
        row = lax.broadcasted_iota(jnp.int32, (8, 128), 0)
        tile = tile + jnp.where(row == 2 * it, res_sq, 0.0) + jnp.where(row == 2 * it + 1, upd_sq, 0.0)

        def spot(s, at):
            return fin.at[at] if last else full.at[it + 1, s, at]

        if last:
            fin[mine, :] = updated
        else:
            full[it + 1, ms, mine, :] = updated
        if last:
            stat[0] = tile

        def zst_copy(k):
            return rcopy(stat.at[0], zsr.at[k], zst, 0, k, term_dev(k))

        def xst_copy(j):
            return rcopy(stat.at[1], xsr.at[j], xst, 0, j, xy_dev(j))

        def zg_copy(k):
            return rcopy(spot(ms, mine), spot(ms, mine), zg, it, (it, k), z_dev(k))

        def zg_in(k):
            here = spot(ms, piece(mc, z_from(k)))
            return rcopy(here, here, zg, it, (it, k), z_dev(k))

        def xg_copy(j, k):
            here = spot(ms, piece(mc, z_from(k)))
            return rcopy(here, here, xg, it, (it, j, k), xy_dev(j))

        def xg_in(j, k):
            here = spot(sec_from(j), piece(mc, z_from(k)))
            return rcopy(here, here, xg, it, (it, j, k), xy_dev(j))

        def cg_copy(j, k):
            here = spot(sec_from(j), piece(mc, z_from(k)))
            return rcopy(here, here, cg, it, (it, j), core_dev)

        def cg_in(j):
            here = spot(sec_from(j), half(1 - mc))
            return rcopy(here, here, cg, it, (it, j), core_dev)

        def spread(k):
            if not last:
                each(1, S, lambda j: xg_copy(j, k).start())
            cg_copy(0, k).start()

        if last:
            for k in range(1, T):
                zst_copy(k).start()
        each(1, Z, lambda k: zg_copy(k).start())
        spread(0)
        if last:
            for k in range(1, T):
                zst_copy(k).wait_recv()
                tile = tile + zsr[k]
            stat[1] = tile
            each(1, S, lambda j: xst_copy(j).start())

        def relay_z(k):
            zg_in(k).wait_recv()
            spread(k)

        each(1, Z, relay_z)

        if not last:
            def relay_xy(k):
                def one(j):
                    xg_in(j, k).wait_recv()
                    cg_copy(j, k).start()

                each(1, S, one)

            each(0, Z, relay_xy)

        if last:
            for j in range(1, S):
                xst_copy(j).wait_recv()
                tile = tile + xsr[j]
            scale = jnp.ones((1, 1), F32)
            for n in range(iters):
                norms[n] = (scale * jnp.sqrt(tile[2 * n : 2 * n + 1, 0:1]))[0, 0]
                mean = tile[2 * n + 1 : 2 * n + 2, 0:1] / count
                scale = scale / jnp.sqrt(scale * scale * mean + 1e-06)
            cg_in(0).wait_recv()
            out[0] = fin[...] * scale
        else:
            def arrive(j):
                cg_in(j).wait_recv()
                s = sec_from(j)
                split_rows(lambda at: full[it + 1, s, at, :], psi, s)

            each(0, S, arrive)

        def sent(size, kind, at):
            rcopy(size, size, kind, at, kind_at[len(kind[1].shape)], core_dev).wait_send()

        kind_at = {1: 0, 2: (0, 0), 3: (0, 0, 0)}
        others = part.at[0, pl.ds(0, S - 1)]
        rows_out = zsum.at[pl.ds(0, Z - 1)]
        if it == 0:
            sent(others, g0, 0)
            sent(others, f0, 0)
        sent(part.at[1], p1, it)
        sent(others, p2, it)
        sent(rows_out, p3, it)
        sent(rows_out, zg, it)
        if last:
            sent(part.at[0, 0], cg, it)
            sent(zsr.at[pl.ds(0, T - 1)], zst, 0)
            sent(xsr.at[pl.ds(0, S - 1)], xst, 0)
        else:
            sent(others, xg, it)
            sent(part.at[0], cg, it)


def per_device(S, T, wavefunction, left_env, right_env, in_sector, out_sector, precond, shifts):
    n_task, B = left_env.shape[0], left_env.shape[-1]
    iters = shifts.shape[0]
    Z, H = T // 2, B // 2
    R = H // Z
    dma = pltpu.SemaphoreType.DMA
    vmem = pl.BlockSpec(memory_space=pltpu.VMEM)
    smem = pl.BlockSpec(memory_space=pltpu.SMEM)
    hbm = pl.BlockSpec(memory_space=pl.ANY)
    sem_shapes = [
        (1,), (S,), (1,), (S,), (iters,), (iters, S), (iters,), (iters, Z), (iters,), (iters, Z),
        (iters,), (iters, Z), (iters,), (iters, S, Z), (iters,), (iters, S), (1,), (T,), (1,), (S,),
    ]
    return pl.pallas_call(
        functools.partial(kernel, S, T),
        out_shape=(
            jax.ShapeDtypeStruct((1, B, B), F32),
            jax.ShapeDtypeStruct((iters,), F32),
        ),
        in_specs=[smem, smem, smem, vmem, vmem, hbm, hbm],
        out_specs=(vmem, smem),
        scratch_shapes=[
            pltpu.VMEM((2, n_task, B, B), F32),
            pltpu.VMEM((2, 2, n_task, B, B), BF16),
            pltpu.VMEM((iters, S, B, B), F32),
            pltpu.VMEM((B, B), F32),
            pltpu.VMEM((2, S, B, B), BF16),
            pltpu.VMEM((2, n_task, B, B), BF16),
            pltpu.VMEM((n_task, B, B), F32),
            pltpu.VMEM((2, S, H, B), F32),
            pltpu.VMEM((iters, S, H, B), F32),
            pltpu.VMEM((iters, Z, S, R, B), F32),
            pltpu.VMEM((Z, R, B), F32),
            pltpu.VMEM((iters, Z, R, B), F32),
            pltpu.VMEM((2, 8, 128), F32),
            pltpu.VMEM((T, 8, 128), F32),
            pltpu.VMEM((S, 8, 128), F32),
            dma((2, n_task)),
        ]
        + [dma(shape) for shape in sem_shapes],
        compiler_params=pltpu.CompilerParams(
            collective_id=0, has_side_effects=True, vmem_limit_bytes=62 * 1024 * 1024
        ),
    )(in_sector, out_sector, shifts, wavefunction, precond, left_env, right_env)


def solution(mesh):
    placed = (
        P("sector", None, None),
        P(("sector", "term"), None, None),
        P(("sector", "term"), None, None),
        P(("sector", "term")),
        P(("sector", "term")),
        P("sector", None, None),
        P(),
    )
    return jax.shard_map(
        functools.partial(per_device, mesh.shape["sector"], mesh.shape["term"]),
        mesh=mesh,
        in_specs=placed,
        out_specs=(P("sector", None, None), P()),
        check_vma=False,
    )
```

```python
import functools

import jax
import jax.numpy as jnp
from jax import lax
from jax.experimental import pallas as pl
from jax.experimental.pallas import tpu as pltpu
from jax.sharding import PartitionSpec as P

F32 = jnp.float32
BF16 = jnp.bfloat16


def split(x):
    hi = x.astype(BF16)
    return hi, (x - hi.astype(F32)).astype(BF16)


def rcopy(src, dst, sems, out_at, in_at, dev):
    return pltpu.make_async_remote_copy(
        src_ref=src,
        dst_ref=dst,
        send_sem=sems[0].at[out_at],
        recv_sem=sems[1].at[in_at],
        device_id=dev,
        device_id_type=pl.DeviceIdType.MESH,
    )


def each(start, stop, body):
    if stop - start <= 4:
        for i in range(start, stop):
            body(i)
    else:
        lax.fori_loop(start, stop, lambda i, _: (body(i), 0)[1], 0)


def kernel(
    S, T,
    in_s, out_s, shifts, wf, pre, left, right,
    out, norms,
    stage, env, full, fin, psi, mid, res, part, p1r, p2r, zsum, p3r, stat, zsr, xsr,
    esem, *sems,
):
    g0, f0, p1, p2, p3, zg, xg, cg, zst, xst = [
        (sems[2 * i], sems[2 * i + 1]) for i in range(len(sems) // 2)
    ]
    n_task, B = left.shape[0], wf.shape[-1]
    iters = norms.shape[0]
    Z, H = T // 2, B // 2
    R = H // Z
    count = S * B * B
    ms, mt = lax.axis_index("sector"), lax.axis_index("term")
    mz, mc = mt // 2, lax.rem(mt, 2)

    def sec_to(k):
        return lax.rem(ms + k, S)

    def sec_from(k):
        return lax.rem(ms + S - k, S)

    def z_to(k):
        return lax.rem(mz + k, Z)

    def z_from(k):
        return lax.rem(mz + Z - k, Z)

    def xy_dev(k):
        return (sec_to(k), mt)

    def far(k):
        return lax.rem(jnp.where(mz < Z // 2, Z - k, k), Z)

    def z_dev(k):
        return (ms, z_to(k) * 2 + mc)

    def term_dev(k):
        return (ms, lax.rem(mt + k, T))

    core_dev = (ms, mz * 2 + 1 - mc)

    def half(c):
        return pl.ds(pl.multiple_of(c * H, H), H)

    def piece(c, z):
        return pl.ds(pl.multiple_of(c * H + z * R, R), R)

    def zrows(z):
        return pl.ds(pl.multiple_of(z * R, R), R)

    def env_copy(which, t):
        src = left if which == 0 else right
        return pltpu.make_async_copy(src.at[t], stage.at[which, t], esem.at[which, t])

    barrier = pltpu.get_barrier_semaphore()

    def greet(dev):
        pl.semaphore_signal(barrier, inc=1, device_id=dev, device_id_type=pl.DeviceIdType.MESH)

    each(1, S, lambda k: greet(xy_dev(k)))
    for k in range(1, T):
        greet(term_dev(k))

    for which in range(2):
        each(0, n_task, lambda t: env_copy(which, t).start())

    CH = 32

    def split_rows(load, dst, s):
        def rows(i):
            at = pl.ds(pl.multiple_of(i * CH, CH), CH)
            hi, lo = split(load(at))
            dst[0, s, at, :] = hi
            dst[1, s, at, :] = lo

        each(0, B // CH, rows)

    split_rows(lambda at: wf[0, at, :], psi, ms)

    pl.semaphore_wait(barrier, S + T - 2)

    def g0_copy(k):
        return rcopy(wf.at[0, half(mc)], full.at[0, ms, half(mc)], g0, 0, k, xy_dev(k))

    def g0_in(k):
        here = full.at[0, sec_from(k), half(mc)]
        return rcopy(here, here, g0, 0, k, xy_dev(k))

    def f0_copy(k):
        here = full.at[0, sec_from(k), half(mc)]
        return rcopy(here, here, f0, 0, k, core_dev)

    def f0_in(k):
        here = full.at[0, sec_from(k), half(1 - mc)]
        return rcopy(here, here, f0, 0, k, core_dev)

    each(1, S, lambda k: g0_copy(k).start())

    for which in range(2):
        def convert(t):
            env_copy(which, t).wait()
            split_rows(lambda at: stage[which, t, at, :], env.at[which], t)

        each(0, n_task, convert)

    def forward0(k):
        g0_in(k).wait_recv()
        f0_copy(k).start()

    each(1, S, forward0)

    def arrive0(k):
        f0_in(k).wait_recv()
        s = sec_from(k)
        split_rows(lambda at: full[0, s, at, :], psi, s)

    each(1, S, arrive0)

    tile = jnp.zeros((8, 128), F32)
    for it in range(iters):
        last = it == iters - 1

        def first(t):
            s = in_s[t]
            lh, ll = env[0, 0, t], env[0, 1, t]
            ph, plo = psi[0, s], psi[1, s]
            m = jnp.dot(
                jnp.concatenate([lh, ll, lh], axis=1),
                jnp.concatenate([ph, ph, plo], axis=0),
                preferred_element_type=F32,
            )
            mid[0, t], mid[1, t] = split(m)

        def second(t):
            mh, ml = mid[0, t], mid[1, t]
            rh, rl = env[1, 0, t], env[1, 1, t]
            res[t] = jnp.dot(
                jnp.concatenate([mh, ml, mh], axis=1),
                jnp.concatenate([rh, rh, rl], axis=0),
                preferred_element_type=F32,
            )

        for t in range(n_task):
            first(t)
        for t in range(n_task):
            second(t)

        def sums(s, c, dst, extra):
            coef = [jnp.where(out_s[t] == s, 1.0, 0.0).astype(F32) for t in range(n_task)]

            def rows(i):
                at = pl.ds(pl.multiple_of(i * CH, CH), CH)
                src = pl.ds(pl.multiple_of(c * H + i * CH, CH), CH)
                total = coef[0] * res[0, src, :]
                for t in range(1, n_task):
                    total = total + coef[t] * res[t, src, :]
                if extra:
                    total = total + p1r[it, s, at, :]
                part[dst, s, at, :] = total

            each(0, H // CH, rows)

        def p1_copy(s):
            return rcopy(part.at[1, s], p1r.at[it, s], p1, it, (it, s), core_dev)

        def to_partner(k):
            s = sec_to(k)
            sums(s, 1 - mc, 1, False)
            p1_copy(s).start()

        each(1, S + 1, to_partner)

        def p2_copy(j, k):
            return rcopy(
                part.at[0, sec_to(j), zrows(z_to(k))], p2r.at[it, k, j], p2, it, (it, k), xy_dev(j)
            )

        def to_owner(j):
            s = sec_to(j)
            p1_copy(s).wait_recv()
            sums(s, mc, 0, True)

        each(1, S, to_owner)
        for k in range(1, Z + 1):
            each(1, S, lambda j: p2_copy(j, far(k)).start())
        p1_copy(ms).wait_recv()
        sums(ms, mc, 0, True)

        def piece_sum(k):
            total = part[0, ms, zrows(z_to(k)), :]
            here = p2r.at[it, k, pl.ds(1, S - 1)]
            rcopy(here, here, p2, it, (it, k), xy_dev(1)).wait_recv()
            for j in range(1, S):
                total = total + p2r[it, k, j]
            return total

        def p3_copy(k):
            return rcopy(zsum.at[k], p3r.at[it, k], p3, it, (it, k), z_dev(k))

        def to_z(k):
            zsum[k] = piece_sum(k)
            p3_copy(k).start()

        each(1, Z, lambda k: to_z(far(k)))
        sigma = piece_sum(0)
        for k in range(1, Z):
            p3_copy(k).wait_recv()
            sigma = sigma + p3r[it, k]

        mine = piece(mc, mz)
        shift = shifts[it]
        prev = wf[0, mine, :] if it == 0 else full[it, ms, mine, :]
        residual = sigma - shift * prev
        updated = prev - residual / (pre[0, mine, :] - shift)
        res_sq = jnp.sum(residual * residual, axis=(0, 1), keepdims=True)
        upd_sq = jnp.sum(updated * updated, axis=(0, 1), keepdims=True)
        row = lax.broadcasted_iota(jnp.int32, (8, 128), 0)
        tile = tile + jnp.where(row == 2 * it, res_sq, 0.0) + jnp.where(row == 2 * it + 1, upd_sq, 0.0)

        def spot(s, at):
            return fin.at[at] if last else full.at[it + 1, s, at]

        if last:
            fin[mine, :] = updated
        else:
            full[it + 1, ms, mine, :] = updated
        if last:
            stat[0] = tile

        def zst_copy(k):
            return rcopy(stat.at[0], zsr.at[k], zst, 0, k, term_dev(k))

        def xst_copy(j):
            return rcopy(stat.at[1], xsr.at[j], xst, 0, j, xy_dev(j))

        def zg_copy(k):
            return rcopy(spot(ms, mine), spot(ms, mine), zg, it, (it, k), z_dev(k))

        def zg_in(k):
            here = spot(ms, piece(mc, z_from(k)))
            return rcopy(here, here, zg, it, (it, k), z_dev(k))

        def xg_copy(j, k):
            here = spot(ms, piece(mc, z_from(k)))
            return rcopy(here, here, xg, it, (it, j, k), xy_dev(j))

        def xg_in(j, k):
            here = spot(sec_from(j), piece(mc, z_from(k)))
            return rcopy(here, here, xg, it, (it, j, k), xy_dev(j))

        def cg_copy(j, k):
            here = spot(sec_from(j), piece(mc, z_from(k)))
            return rcopy(here, here, cg, it, (it, j), core_dev)

        def cg_in(j):
            here = spot(sec_from(j), half(1 - mc))
            return rcopy(here, here, cg, it, (it, j), core_dev)

        def spread(k):
            if not last:
                each(1, S, lambda j: xg_copy(j, k).start())
            cg_copy(0, k).start()

        if last:
            for k in range(1, T):
                zst_copy(k).start()
        each(1, Z, lambda k: zg_copy(far(k)).start())
        spread(0)
        if last:
            for k in range(1, T):
                zst_copy(k).wait_recv()
                tile = tile + zsr[k]
            stat[1] = tile
            each(1, S, lambda j: xst_copy(j).start())

        def relay_z(k):
            zg_in(k).wait_recv()
            spread(k)

        each(1, Z, lambda k: relay_z(far(k)))

        if not last:
            def relay_xy(k):
                def one(j):
                    xg_in(j, k).wait_recv()
                    cg_copy(j, k).start()

                each(1, S, one)

            relay_xy(0)
            each(1, Z, lambda k: relay_xy(far(k)))

        if last:
            for j in range(1, S):
                xst_copy(j).wait_recv()
                tile = tile + xsr[j]
            scale = jnp.ones((1, 1), F32)
            for n in range(iters):
                norms[n] = (scale * jnp.sqrt(tile[2 * n : 2 * n + 1, 0:1]))[0, 0]
                mean = tile[2 * n + 1 : 2 * n + 2, 0:1] / count
                scale = scale / jnp.sqrt(scale * scale * mean + 1e-06)
            cg_in(0).wait_recv()
            out[0] = fin[...] * scale
        else:
            def arrive(j):
                cg_in(j).wait_recv()
                s = sec_from(j)
                split_rows(lambda at: full[it + 1, s, at, :], psi, s)

            each(0, S, arrive)

        def sent(size, kind, at):
            rcopy(size, size, kind, at, kind_at[len(kind[1].shape)], core_dev).wait_send()

        kind_at = {1: 0, 2: (0, 0), 3: (0, 0, 0)}
        others = part.at[0, pl.ds(0, S - 1)]
        rows_out = zsum.at[pl.ds(0, Z - 1)]
        if it == 0:
            sent(others, g0, 0)
            sent(others, f0, 0)
        sent(part.at[1], p1, it)
        sent(others, p2, it)
        sent(rows_out, p3, it)
        sent(rows_out, zg, it)
        if last:
            sent(part.at[0, 0], cg, it)
            sent(zsr.at[pl.ds(0, T - 1)], zst, 0)
            sent(xsr.at[pl.ds(0, S - 1)], xst, 0)
        else:
            sent(others, xg, it)
            sent(part.at[0], cg, it)


def per_device(S, T, wavefunction, left_env, right_env, in_sector, out_sector, precond, shifts):
    n_task, B = left_env.shape[0], left_env.shape[-1]
    iters = shifts.shape[0]
    Z, H = T // 2, B // 2
    R = H // Z
    dma = pltpu.SemaphoreType.DMA
    vmem = pl.BlockSpec(memory_space=pltpu.VMEM)
    smem = pl.BlockSpec(memory_space=pltpu.SMEM)
    hbm = pl.BlockSpec(memory_space=pl.ANY)
    sem_shapes = [
        (1,), (S,), (1,), (S,), (iters,), (iters, S), (iters,), (iters, Z), (iters,), (iters, Z),
        (iters,), (iters, Z), (iters,), (iters, S, Z), (iters,), (iters, S), (1,), (T,), (1,), (S,),
    ]
    return pl.pallas_call(
        functools.partial(kernel, S, T),
        out_shape=(
            jax.ShapeDtypeStruct((1, B, B), F32),
            jax.ShapeDtypeStruct((iters,), F32),
        ),
        in_specs=[smem, smem, smem, vmem, vmem, hbm, hbm],
        out_specs=(vmem, smem),
        scratch_shapes=[
            pltpu.VMEM((2, n_task, B, B), F32),
            pltpu.VMEM((2, 2, n_task, B, B), BF16),
            pltpu.VMEM((iters, S, B, B), F32),
            pltpu.VMEM((B, B), F32),
            pltpu.VMEM((2, S, B, B), BF16),
            pltpu.VMEM((2, n_task, B, B), BF16),
            pltpu.VMEM((n_task, B, B), F32),
            pltpu.VMEM((2, S, H, B), F32),
            pltpu.VMEM((iters, S, H, B), F32),
            pltpu.VMEM((iters, Z, S, R, B), F32),
            pltpu.VMEM((Z, R, B), F32),
            pltpu.VMEM((iters, Z, R, B), F32),
            pltpu.VMEM((2, 8, 128), F32),
            pltpu.VMEM((T, 8, 128), F32),
            pltpu.VMEM((S, 8, 128), F32),
            dma((2, n_task)),
        ]
        + [dma(shape) for shape in sem_shapes],
        compiler_params=pltpu.CompilerParams(
            collective_id=0, has_side_effects=True, vmem_limit_bytes=62 * 1024 * 1024
        ),
    )(in_sector, out_sector, shifts, wavefunction, precond, left_env, right_env)


def solution(mesh):
    placed = (
        P("sector", None, None),
        P(("sector", "term"), None, None),
        P(("sector", "term"), None, None),
        P(("sector", "term")),
        P(("sector", "term")),
        P("sector", None, None),
        P(),
    )
    return jax.shard_map(
        functools.partial(per_device, mesh.shape["sector"], mesh.shape["term"]),
        mesh=mesh,
        in_specs=placed,
        out_specs=(P("sector", None, None), P()),
        check_vma=False,
    )
```
